256 devices in a mesh: sta: 64 (over z, x, core), evt: 4 (over y).
Axes of the slice: x: 4, y: 4, z: 8, core: 2. Of those that a mesh axis runs over, the one named last changes fastest.
Arguments:
- waveforms: bfloat16 [1024, 512, 1024], P(('evt', 'sta')), may hold values from -18 to 18
- pair_events: int32 [4096, 2], P('evt'), may hold values from 0 to 1023, as said below
- pair_valid: int32 [4096], P('evt'), may hold values from 0 to 1, as said below
- presence: int32 [1024, 512], P(None, 'sta'), may hold values 0 or 1
Outputs:
- correlation: bfloat16 [4096, 512, 256], P('evt', 'sta')
- pair_peak: float32 [4096], P('evt')
The draws below stay inside these ranges and needn't reach their ends.
Inputs may be any that keep to these rules, and one draw needn't show every extreme that they name: `pair_events`: slot rows p * 1024 to (p + 1) * 1024 - 1 belong to block p; each row names first an event of block p (events p * 256 to (p + 1) * 256 - 1), then a different event at most 128 positions away from it; in every block the first row names the block's first event and the second row the block's last event, each with an event exactly 128 away. `pair_valid`: in each block of 1024 slots the valid slots come first; in every draw some block is full.
All inputs are finite; a program needn't handle non-finite values. No bound on the sum of `presence` on one device may be relied on, other than what follows from the above.
Results may differ from the reference program's by a relative error of at most 0.0064.
Values may be sent and summed in bfloat16 or wider, within the bound.
A program may use at most 64 MiB of HBM per device.

```python
import math
import jax
import jax.numpy as jnp
from jax import lax

WIN = 1024
LAGS = 256
EVT_DEV = 4
PAIR_CAP = 1024
STATIONS = 512
BLOCK = 256
BAND = 128
EVENTS = 1024
PAIRS = 4096


def draw_waveforms(key, part):
    subkeys = jax.random.split(jax.random.fold_in(key, 11), 5)
    station_base = jax.random.truncated_normal(subkeys[0], -4.0, 4.0, (STATIONS, WIN), jnp.float32)
    event_delay = jax.random.randint(subkeys[1], (EVENTS, 1, 1), 0, LAGS // 4)
    sample_index = jnp.arange(WIN, dtype=jnp.int32)[None, None, :]
    source_index = (sample_index - event_delay) % WIN
    station_rows = jnp.arange(STATIONS, dtype=jnp.int32)[None, :, None]
    shifted = station_base[station_rows, source_index]
    coherence_ramp = 0.3 + 0.65 * jnp.arange(STATIONS, dtype=jnp.float32) / STATIONS
    coherence = jnp.minimum(coherence_ramp[None, :, None] * jax.random.uniform(subkeys[2], (1, STATIONS, 1), jnp.float32, 0.9, 1.1), 0.95)
    noise_part = jax.random.truncated_normal(subkeys[3], -4.0, 4.0, (EVENTS, STATIONS, WIN), jnp.float32)
    amplitude = jnp.exp(jax.random.uniform(subkeys[4], (EVENTS, STATIONS, 1), jnp.float32, math.log(0.3), math.log(3.0)))
    return (amplitude * (coherence * shifted + jnp.sqrt(1.0 - coherence * coherence) * noise_part)).astype(jnp.bfloat16)


def draw_pair_events(key, part):
    subkeys = jax.random.split(jax.random.fold_in(key, 17), 3)
    slot_index = jnp.arange(PAIRS, dtype=jnp.int32)
    owner_block = slot_index // PAIR_CAP
    slot_in_block = slot_index % PAIR_CAP
    first_event = owner_block * BLOCK + jax.random.randint(subkeys[0], (PAIRS,), 0, BLOCK)
    first_event = jnp.where(slot_in_block == 0, owner_block * BLOCK, first_event)
    first_event = jnp.where(slot_in_block == 1, owner_block * BLOCK + BLOCK - 1, first_event)
    distance = jax.random.randint(subkeys[1], (PAIRS,), 1, BAND + 1)
    distance = jnp.where(slot_in_block < 2, BAND, distance)
    direction = jnp.where(jax.random.randint(subkeys[2], (PAIRS,), 0, 2) == 0, -1, 1)
    direction = jnp.where(slot_in_block == 0, -1, direction)
    direction = jnp.where(slot_in_block == 1, 1, direction)
    second_event = first_event + direction * distance
    outside = (second_event < 0) | (second_event >= EVENTS)
    second_event = jnp.where(outside, first_event - direction * distance, second_event)
    return jnp.stack([first_event, second_event], axis=1).astype(jnp.int32)


def draw_pair_valid(key, part):
    subkeys = jax.random.split(jax.random.fold_in(key, 23), 2)
    owners = PAIRS // PAIR_CAP
    filled = jax.random.randint(subkeys[0], (owners,), PAIR_CAP // 4, PAIR_CAP + 1)
    full_owner = jax.random.randint(subkeys[1], (), 0, owners)
    filled = jnp.where(jnp.arange(owners, dtype=jnp.int32) == full_owner, PAIR_CAP, filled)
    slot_index = jnp.arange(PAIRS, dtype=jnp.int32)
    return (slot_index % PAIR_CAP < filled[slot_index // PAIR_CAP]).astype(jnp.int32)


def place_ends(drawn, own_key, least, largest):
    spot = [jax.random.randint(jax.random.fold_in(own_key, axis), (), 0, length) for axis, length in enumerate(drawn.shape)]
    widest = drawn.shape.index(max(drawn.shape))
    neighbour = spot[:widest] + [(spot[widest] + 1) % drawn.shape[widest]] + spot[widest + 1:]
    return drawn.at[tuple(spot)].set(least).at[tuple(neighbour)].set(largest)


def setup_inputs(seed: int = 0) -> dict:
    key_of = jax.random.split(jax.random.key(seed), 5)
    waveforms = draw_waveforms(jax.random.fold_in(key_of[4], 71), 0)
    pair_events = draw_pair_events(jax.random.fold_in(key_of[4], 71), 0)
    pair_valid = draw_pair_valid(jax.random.fold_in(key_of[4], 71), 0)
    presence = place_ends((jax.random.randint(key_of[3], (EVENTS, STATIONS), 0, 4) < 3).astype(jnp.int32), jax.random.fold_in(key_of[3], 1), 0, 1)
    return {"waveforms": waveforms, "pair_events": pair_events, "pair_valid": pair_valid, "presence": presence}


def spectral_tables(window, lag_count):
    half_width = window // 2
    sample_index = jnp.arange(window, dtype=jnp.int32)
    bin_index = jnp.arange(half_width, dtype=jnp.int32)
    phase_angle = (sample_index[:, None] * bin_index[None, :] % window).astype(jnp.float32) * (2.0 * math.pi / window)
    forward = (jnp.concatenate([jnp.cos(phase_angle), -jnp.sin(phase_angle)], axis=1) / math.sqrt(window)).astype(jnp.bfloat16)
    shifts = jnp.arange(lag_count, dtype=jnp.int32) - lag_count // 2
    lag_angle = (bin_index[:, None] * shifts[None, :] % window).astype(jnp.float32) * (2.0 * math.pi / window)
    factor = jnp.where(bin_index == 0, 1.0, 2.0).astype(jnp.float32)
    inverse = jnp.concatenate([factor[:, None] * jnp.cos(lag_angle), -factor[:, None] * jnp.sin(lag_angle)], axis=0).astype(jnp.bfloat16)
    energy_weights = jnp.concatenate([factor, factor])
    return (forward, inverse, energy_weights)

def to_spectra(traces, forward):
    flattened = traces.reshape(-1, traces.shape[-1])
    result = jnp.dot(flattened, forward, preferred_element_type=jnp.float32).astype(jnp.bfloat16)
    return result.reshape(traces.shape[:-1] + (forward.shape[1],))

def pair_group(spectra, energy, presence, inverse, first_event, second_event, valid_rows):
    window = spectra.shape[-1]
    half_width = window // 2
    first_spec = jnp.take(spectra, first_event, axis=0).astype(jnp.float32)
    second_spec = jnp.take(spectra, second_event, axis=0).astype(jnp.float32)
    first_real, first_imag = (first_spec[..., :half_width], first_spec[..., half_width:])
    second_real, second_imag = (second_spec[..., :half_width], second_spec[..., half_width:])
    cross_spec = jnp.concatenate([first_real * second_real + first_imag * second_imag, first_real * second_imag - first_imag * second_real], axis=-1).astype(jnp.bfloat16)
    group_rows, station_share = (cross_spec.shape[0], cross_spec.shape[1])
    lagged = jnp.dot(cross_spec.reshape(-1, window), inverse, preferred_element_type=jnp.float32)
    lagged = lagged.reshape(group_rows, station_share, inverse.shape[1])
    norm_factor = lax.rsqrt(jnp.take(energy, first_event, axis=0) * jnp.take(energy, second_event, axis=0))
    weight_mask = valid_rows[:, None].astype(jnp.float32) * jnp.take(presence, first_event, axis=0).astype(jnp.float32) * jnp.take(presence, second_event, axis=0).astype(jnp.float32)
    normalized = lagged * (norm_factor * weight_mask)[:, :, None]
    peak_terms = lax.optimization_barrier(jnp.sum(lax.optimization_barrier(jnp.max(normalized, axis=-1)) * weight_mask, axis=-1))
    present = lax.optimization_barrier(jnp.sum(weight_mask, axis=-1))
    return (normalized.astype(jnp.bfloat16), peak_terms, present)

def reference(waveforms, pair_events, pair_valid, presence):
    forward, inverse, energy_weights = spectral_tables(WIN, LAGS)
    grouped = waveforms.reshape(EVENTS // EVT_DEV, EVT_DEV, STATIONS, WIN)
    spectra = lax.map(lambda traces: to_spectra(traces, forward), grouped).reshape(EVENTS, STATIONS, WIN)
    energy = lax.map(lambda piece: lax.optimization_barrier(jnp.sum(energy_weights * jnp.square(piece.astype(jnp.float32)), axis=-1)) + 1e-06, spectra.reshape(EVENTS // EVT_DEV, EVT_DEV, STATIONS, WIN)).reshape(EVENTS, STATIONS)
    group_rows = min(128, PAIR_CAP)
    event_groups = pair_events.reshape(PAIRS // group_rows, group_rows, 2)
    valid_groups = pair_valid.reshape(PAIRS // group_rows, group_rows)

    def one_group(group_item):
        events_here, valid_rows = group_item
        return pair_group(spectra, energy, presence, inverse, events_here[:, 0], events_here[:, 1], valid_rows)
    correlation, peak_terms, present = lax.map(one_group, (event_groups, valid_groups))
    pair_peak = peak_terms.reshape(PAIRS) / jnp.maximum(present.reshape(PAIRS), 1.0)
    return (correlation.reshape(PAIRS, STATIONS, LAGS), pair_peak)
```

```python
import functools
import math

import jax
import jax.numpy as jnp
import numpy as np
from jax import lax
from jax.experimental import pallas as pl
from jax.experimental.pallas import tpu as pltpu
from jax.sharding import PartitionSpec as P

LAGS = 256
MESH = pl.DeviceIdType.MESH
LANES = 128


def spectral_tables(window, lag_count):
    half_width = window // 2
    bins = np.arange(half_width)
    phase = (np.arange(window)[:, None] * bins[None, :] % window) * (2.0 * math.pi / window)
    forward = np.concatenate([np.cos(phase), -np.sin(phase)], axis=1) / math.sqrt(window)
    shifts = np.arange(lag_count) - lag_count // 2
    angle = (bins[:, None] * shifts[None, :] % window) * (2.0 * math.pi / window)
    factor = np.where(bins == 0, 1.0, 2.0)[:, None]
    inverse = np.concatenate([factor * np.cos(angle), -factor * np.sin(angle)], axis=0)
    return forward.astype(np.float32).astype(jnp.bfloat16), inverse.astype(np.float32).astype(jnp.bfloat16)


def gather_kernel(
    w_ref, table_hbm, presence_ref, spec_ref, scale_ref,
    raw, table, send_sem, recv_sem, up_send, up_recv, local_sem,
):
    me = lax.axis_index("sta")
    row = lax.axis_index("evt")
    rows = lax.axis_size("evt")
    z, x, c = me // 8, (me // 2) % 4, me % 2

    def target(k):
        dz, dx, dc = (3 * k) % 8, k // 16, (k // 8) % 2
        return ((z + dz) % 8) * 8 + ((x + dx) % 4) * 2 + (c + dc) % 2

    def source(k):
        dz, dx, dc = (3 * k) % 8, k // 16, (k // 8) % 2
        return ((z + 8 - dz) % 8) * 8 + ((x + 4 - dx) % 4) * 2 + (c + dc) % 2

    def send(k):
        to = target(k)
        return pltpu.make_async_remote_copy(
            src_ref=w_ref.at[:, pl.ds(pl.multiple_of(to * 8, 8), 8), :],
            dst_ref=raw.at[me],
            send_sem=send_sem.at[k],
            recv_sem=recv_sem.at[k],
            device_id={"sta": to},
            device_id_type=MESH,
        )

    def forward(k):
        s = source(k)
        side = jnp.where(s < 32, rows - 1, 1)
        return pltpu.make_async_remote_copy(
            src_ref=raw.at[s],
            dst_ref=raw.at[64 + s],
            send_sem=up_send.at[k],
            recv_sem=up_recv.at[k],
            device_id={"evt": (row + side) % rows},
            device_id_type=MESH,
        )

    fetch = pltpu.make_async_copy(table_hbm, table, local_sem.at[0])
    fetch.start()
    own = pltpu.make_async_copy(
        w_ref.at[:, pl.ds(pl.multiple_of(me * 8, 8), 8), :], raw.at[me], local_sem.at[1]
    )
    own.start()
    barrier = pltpu.get_barrier_semaphore()

    @pl.loop(1, 64)
    def _(k):
        pl.semaphore_signal(barrier, inc=1, device_id={"sta": target(k)}, device_id_type=MESH)

    for side in (1, rows - 1):
        pl.semaphore_signal(
            barrier, inc=1, device_id={"evt": (row + side) % rows}, device_id_type=MESH
        )
    pl.semaphore_wait(barrier, 65)

    @pl.loop(1, 64)
    def _(k):
        send(k).start()

    lane = lax.broadcasted_iota(jnp.int32, (1, 256), 1)
    lane_one = lax.broadcasted_iota(jnp.int32, (8, LANES), 1)

    def transform(slots):
        block = jnp.concatenate([raw[s].reshape(32, 1024) for s in slots], axis=0)
        power = jnp.zeros((256, LANES), jnp.float32)
        for n in range(4):
            y = jnp.dot(block, table[:, n * 256 : (n + 1) * 256], preferred_element_type=jnp.float32)
            y = y.astype(jnp.bfloat16)
            for i, s in enumerate(slots):
                spec_ref[pl.ds(s * 4, 4), :, n * 256 : (n + 1) * 256] = y[i * 32 : i * 32 + 32].reshape(4, 8, 256)
            y = y.astype(jnp.float32)
            weight = 2.0 if n % 2 else jnp.where(lane == 0, 1.0, 2.0)
            y = y * y * weight
            power = power + y[:, :LANES] + y[:, LANES:]
        energy = jnp.sum(power, axis=1, keepdims=True) + 1e-06
        scale = jnp.broadcast_to(lax.rsqrt(energy), (256, LANES)).reshape(8, 4, 8, LANES)
        for i, s in enumerate(slots):
            tile = presence_ref[:, pl.ds(pl.multiple_of(s // 32 * LANES, LANES), LANES)]
            for e in range(4):
                here = jnp.where(lane_one == (s % 32) * 4 + e, tile, 0.0)
                scale_ref[s * 4 + e] = scale[i, e] * jnp.sum(here, axis=1, keepdims=True)

    def own_batch(j):
        transform([source(8 * j + i) for i in range(8)])

    def halo_batch(j):
        for i in range(8):
            forward(8 * j + i).wait_recv()
        transform([64 + source(8 * j + i) for i in range(8)])

    fetch.wait()

    @pl.loop(0, 8)
    def _(j):
        @pl.loop(0, 8)
        def _(i):
            k = 8 * j + i

            @pl.when(k == 0)
            def _():
                own.wait()

            @pl.when(k > 0)
            def _():
                send(k).wait_recv()

            forward(k).start()

        own_batch(j)

        @pl.when(j > 0)
        def _():
            halo_batch(j - 1)

    halo_batch(7)
    scale_ref[pl.ds(512, 8)] = jnp.zeros((8, 8, LANES), jnp.float32)

    @pl.loop(1, 64)
    def _(k):
        send(k).wait_send()

    @pl.loop(0, 64)
    def _(k):
        forward(k).wait_send()


GROUP = 128


def pair_kernel(first_ref, second_ref, mark_ref, spec_ref, scale_ref, inverse_ref, out_ref, stat_ref, cross, factor):
    base = pl.program_id(0) * GROUP

    @pl.loop(0, GROUP // 2)
    def _(i):
        tiles = []
        for q in range(2):
            p = base + 2 * i + q
            a, b, m = first_ref[p], second_ref[p], mark_ref[p]
            factor[2 * i + q] = scale_ref[m] * scale_ref[b]
            xa = spec_ref[a].astype(jnp.float32)
            xb = spec_ref[b].astype(jnp.float32)
            ra, ia, rb, ib = xa[:, :512], xa[:, 512:], xb[:, :512], xb[:, 512:]
            tiles.append(jnp.concatenate([ra * rb + ia * ib, ra * ib - ia * rb], axis=1))
        cross[pl.ds(pl.multiple_of(i * 16, 16), 16), :] = jnp.concatenate(tiles, axis=0).astype(jnp.bfloat16)

    lane = lax.broadcasted_iota(jnp.int32, (1, 1, LANES), 2)
    peaks = jnp.zeros((8, LANES), jnp.float32)
    counts = jnp.zeros((8, LANES), jnp.float32)
    step = 32
    for t in range(GROUP // step):
        y = jnp.dot(cross[t * step * 8 : (t + 1) * step * 8, :], inverse_ref[...], preferred_element_type=jnp.float32)
        y = y.reshape(step, 8, LAGS)
        f = factor[t * step : (t + 1) * step]
        lo, hi = y[:, :, :LANES] * f, y[:, :, LANES:] * f
        out_ref[t * step : (t + 1) * step, :, :LANES] = lo.astype(jnp.bfloat16)
        out_ref[t * step : (t + 1) * step, :, LANES:] = hi.astype(jnp.bfloat16)
        top = jnp.max(jnp.maximum(lo, hi), axis=2, keepdims=True)
        here = lane == lax.broadcasted_iota(jnp.int32, (step, 1, 1), 0) + t * step
        peaks = peaks + jnp.sum(jnp.where(here, top, 0.0), axis=0)
        counts = counts + jnp.sum(jnp.where(here & (f > 0.0), 1.0, 0.0), axis=0)
    stat_ref[0, 0:1, :] = jnp.sum(peaks, axis=0, keepdims=True)
    stat_ref[0, 1:2, :] = jnp.sum(counts, axis=0, keepdims=True)


def reduce_kernel(stat_ref, out_ref, inbox, sums, send_sem, recv_sem):
    me = lax.axis_index("sta")
    near, far = me % 8, me // 8

    def copy(k, stage):
        if stage == 0:
            to = far * 8 + (near + k) % 8
        else:
            to = (far + k) % 8 * 8 + near
        return pltpu.make_async_remote_copy(
            src_ref=sums.at[stage],
            dst_ref=inbox.at[stage, k],
            send_sem=send_sem.at[stage, k],
            recv_sem=recv_sem.at[stage, k],
            device_id={"sta": to},
            device_id_type=MESH,
        )

    barrier = pltpu.get_barrier_semaphore()
    for k in range(1, 8):
        pl.semaphore_signal(barrier, inc=1, device_id={"sta": far * 8 + (near + k) % 8}, device_id_type=MESH)
        pl.semaphore_signal(barrier, inc=1, device_id={"sta": (far + k) % 8 * 8 + near}, device_id_type=MESH)
    sums[0] = stat_ref[...]
    pl.semaphore_wait(barrier, 14)
    for stage in range(2):
        for k in range(1, 8):
            copy(k, stage).start()
        total = sums[stage]
        for k in range(1, 8):
            copy(k, stage).wait_recv()
            total = total + inbox[stage, k]
        if stage == 0:
            sums[1] = total
    for stage in range(2):
        for k in range(1, 8):
            copy(k, stage).wait_send()
    for g in range(8):
        out_ref[g : g + 1, :] = total[2 * g : 2 * g + 1] / jnp.maximum(total[2 * g + 1 : 2 * g + 2], 1.0)


def body(waveforms, pair_events, pair_valid, presence):
    forward, inverse = spectral_tables(1024, LAGS)
    row = lax.axis_index("evt")
    count = pair_events.shape[0]
    around = jnp.pad(presence.T.astype(jnp.float32), ((0, 0), (128, 128)))
    window = lax.dynamic_slice_in_dim(around, row * 256, 512, axis=1)
    window = jnp.concatenate([window[:, 128:], window[:, :128]], axis=1)
    vmem = pl.BlockSpec(memory_space=pltpu.VMEM)
    hbm = pl.BlockSpec(memory_space=pl.ANY)
    spec, scale = pl.pallas_call(
        gather_kernel,
        out_shape=(
            jax.ShapeDtypeStruct((512, 8, 1024), jnp.bfloat16),
            jax.ShapeDtypeStruct((520, 8, LANES), jnp.float32),
        ),
        in_specs=[hbm, hbm, vmem],
        out_specs=(vmem, vmem),
        scratch_shapes=[
            pltpu.VMEM((128, 4, 8, 1024), jnp.bfloat16),
            pltpu.VMEM((1024, 1024), jnp.bfloat16),
            pltpu.SemaphoreType.DMA((64,)),
            pltpu.SemaphoreType.DMA((64,)),
            pltpu.SemaphoreType.DMA((64,)),
            pltpu.SemaphoreType.DMA((64,)),
            pltpu.SemaphoreType.DMA((2,)),
        ],
        compiler_params=pltpu.CompilerParams(
            collective_id=0, has_side_effects=True, vmem_limit_bytes=40 << 20
        ),
    )(waveforms, jnp.asarray(forward), window)

    slots = (pair_events - row * 256) & 511
    first, second = slots[:, 0], slots[:, 1]
    mark = jnp.where(pair_valid == 1, first, 512)
    correlation, stat = pl.pallas_call(
        pair_kernel,
        out_shape=(
            jax.ShapeDtypeStruct((count, 8, LAGS), jnp.bfloat16),
            jax.ShapeDtypeStruct((count // GROUP, 2, LANES), jnp.float32),
        ),
        grid_spec=pltpu.PrefetchScalarGridSpec(
            num_scalar_prefetch=3,
            grid=(count // GROUP,),
            in_specs=[vmem, vmem, vmem],
            out_specs=(
                pl.BlockSpec((GROUP, 8, LAGS), lambda g, *_: (g, 0, 0)),
                pl.BlockSpec((1, 2, LANES), lambda g, *_: (g, 0, 0)),
            ),
            scratch_shapes=[
                pltpu.VMEM((GROUP * 8, 1024), jnp.bfloat16),
                pltpu.VMEM((GROUP, 8, LANES), jnp.float32),
            ],
        ),
        compiler_params=pltpu.CompilerParams(vmem_limit_bytes=40 << 20),
    )(first, second, mark, spec, scale, jnp.asarray(inverse))

    mean = pl.pallas_call(
        reduce_kernel,
        out_shape=jax.ShapeDtypeStruct((8, LANES), jnp.float32),
        in_specs=[vmem],
        out_specs=vmem,
        scratch_shapes=[
            pltpu.VMEM((2, 8, 16, LANES), jnp.float32),
            pltpu.VMEM((2, 16, LANES), jnp.float32),
            pltpu.SemaphoreType.DMA((2, 8)),
            pltpu.SemaphoreType.DMA((2, 8)),
        ],
        compiler_params=pltpu.CompilerParams(collective_id=1, has_side_effects=True),
    )(stat.reshape(16, LANES))
    return (correlation, mean.reshape(count))


def solution(mesh):
    return jax.shard_map(
        body,
        mesh=mesh,
        in_specs=(P(("evt", "sta"), None, None), P("evt", None), P("evt"), P(None, "sta")),
        out_specs=(P("evt", "sta", None), P("evt")),
        check_vma=False,
    )
```

```python
import functools
import math

import jax
import jax.numpy as jnp
import numpy as np
from jax import lax
from jax.experimental import pallas as pl
from jax.experimental.pallas import tpu as pltpu
from jax.sharding import PartitionSpec as P

LAGS = 256
MESH = pl.DeviceIdType.MESH
LANES = 128


def spectral_tables(window, lag_count):
    half_width = window // 2
    bins = np.arange(half_width)
    phase = (np.arange(window)[:, None] * bins[None, :] % window) * (2.0 * math.pi / window)
    forward = np.concatenate([np.cos(phase), -np.sin(phase)], axis=1) / math.sqrt(window)
    shifts = np.arange(lag_count) - lag_count // 2
    angle = (bins[:, None] * shifts[None, :] % window) * (2.0 * math.pi / window)
    factor = np.where(bins == 0, 1.0, 2.0)[:, None]
    inverse = np.concatenate([factor * np.cos(angle), -factor * np.sin(angle)], axis=0)
    return forward.astype(np.float32).astype(jnp.bfloat16), inverse.astype(np.float32).astype(jnp.bfloat16)


CHUNK = 32


def kernel(
    w_ref, table_hbm, inverse_hbm, event_ref, valid_ref, presence_ref, out_ref, mean_ref,
    raw, table, inverse, spec, scale, cross, factor, tiles, peak_sum, sums, inbox,
    send_sem, recv_sem, up_send, up_recv, local_sem, out_sem, sum_send, sum_recv,
):
    me = lax.axis_index("sta")
    row = lax.axis_index("evt")
    rows = lax.axis_size("evt")
    z, x, c = me // 8, (me // 2) % 4, me % 2

    def target(k):
        dz, dx, dc = (3 * k) % 8, k // 16, (k // 8) % 2
        return ((z + dz) % 8) * 8 + ((x + dx) % 4) * 2 + (c + dc) % 2

    def source(k):
        dz, dx, dc = (3 * k) % 8, k // 16, (k // 8) % 2
        return ((z + 8 - dz) % 8) * 8 + ((x + 4 - dx) % 4) * 2 + (c + dc) % 2

    def send(k):
        to = target(k)
        return pltpu.make_async_remote_copy(
            src_ref=w_ref.at[:, pl.ds(pl.multiple_of(to * 8, 8), 8), :],
            dst_ref=raw.at[me],
            send_sem=send_sem.at[k],
            recv_sem=recv_sem.at[k],
            device_id={"sta": to},
            device_id_type=MESH,
        )

    def forward(k):
        s = source(k)
        side = jnp.where(s < 32, rows - 1, 1)
        return pltpu.make_async_remote_copy(
            src_ref=raw.at[s],
            dst_ref=raw.at[64 + s],
            send_sem=up_send.at[k],
            recv_sem=up_recv.at[k],
            device_id={"evt": (row + side) % rows},
            device_id_type=MESH,
        )

    fetch = pltpu.make_async_copy(table_hbm, table, local_sem.at[0])
    fetch.start()
    own = pltpu.make_async_copy(
        w_ref.at[:, pl.ds(pl.multiple_of(me * 8, 8), 8), :], raw.at[me], local_sem.at[1]
    )
    own.start()
    fetch_inverse = pltpu.make_async_copy(inverse_hbm, inverse, local_sem.at[2])
    fetch_inverse.start()
    barrier = pltpu.get_barrier_semaphore()

    @pl.loop(1, 64)
    def _(k):
        pl.semaphore_signal(barrier, inc=1, device_id={"sta": target(k)}, device_id_type=MESH)

    for side in (1, rows - 1):
        pl.semaphore_signal(
            barrier, inc=1, device_id={"evt": (row + side) % rows}, device_id_type=MESH
        )
    pl.semaphore_wait(barrier, 65)

    @pl.loop(1, 64)
    def _(k):
        send(k).start()

    lane = lax.broadcasted_iota(jnp.int32, (1, 256), 1)
    lane_one = lax.broadcasted_iota(jnp.int32, (8, LANES), 1)

    def transform(slots, first_events):
        block = jnp.concatenate([raw[s].reshape(32, 1024) for s in slots], axis=0)
        power = jnp.zeros((256, LANES), jnp.float32)
        for n in range(4):
            y = jnp.dot(block, table[:, n * 256 : (n + 1) * 256], preferred_element_type=jnp.float32)
            y = y.astype(jnp.bfloat16)
            for i, s in enumerate(slots):
                spec[pl.ds(s * 4, 4), :, n * 256 : (n + 1) * 256] = y[i * 32 : i * 32 + 32].reshape(4, 8, 256)
            y = y.astype(jnp.float32)
            weight = 2.0 if n % 2 else jnp.where(lane == 0, 1.0, 2.0)
            y = y * y * weight
            power = power + y[:, :LANES] + y[:, LANES:]
        energy = jnp.sum(power, axis=1, keepdims=True) + 1e-06
        strength = jnp.broadcast_to(lax.rsqrt(energy), (256, LANES)).reshape(8, 4, 8, LANES)
        for i, (s, event) in enumerate(zip(slots, first_events)):
            tile = presence_ref[:, pl.ds(pl.multiple_of(event // LANES * LANES, LANES), LANES)].astype(jnp.float32)
            for e in range(4):
                here = jnp.where(lane_one == event % LANES + e, tile, 0.0)
                scale[s * 4 + e] = strength[i, e] * jnp.sum(here, axis=1, keepdims=True)

    def own_batch(j):
        slots = [source(8 * j + i) for i in range(8)]
        transform(slots, [row * 256 + 4 * s for s in slots])

    def halo_batch(j):
        for i in range(8):
            forward(8 * j + i).wait_recv()
        slots = [source(8 * j + i) for i in range(8)]
        events = rows * 256
        transform(
            [64 + s for s in slots],
            [(row * 256 + jnp.where(s < 32, 256, events - 256) + 4 * s) % events for s in slots],
        )

    fetch.wait()
    fetch_inverse.wait()

    @pl.loop(0, 8)
    def _(j):
        @pl.loop(0, 8)
        def _(i):
            k = 8 * j + i

            @pl.when(k == 0)
            def _():
                own.wait()

            @pl.when(k > 0)
            def _():
                send(k).wait_recv()

            forward(k).start()

        own_batch(j)

        @pl.when(j > 0)
        def _():
            halo_batch(j - 1)

    halo_batch(7)
    scale[pl.ds(512, 8)] = jnp.zeros((8, 8, LANES), jnp.float32)

    first_event = row * 256
    column = lax.broadcasted_iota(jnp.int32, (1, 1, LANES), 2)
    position = lax.broadcasted_iota(jnp.int32, (CHUNK, 1, 1), 0)
    peak_sum[...] = jnp.zeros_like(peak_sum)

    def put(g):
        span = pl.ds(pl.multiple_of(g * LANES, LANES), LANES)
        return pltpu.make_async_copy(tiles.at[span], out_ref.at[span], out_sem.at[g])

    @pl.loop(0, 1024 // CHUNK)
    def _(t):
        for i in range(CHUNK // 2):
            two = []
            for q in range(2):
                p = t * CHUNK + 2 * i + q
                a = (event_ref[0, p] - first_event) & 511
                b = (event_ref[1, p] - first_event) & 511
                m = jnp.where(valid_ref[p] == 1, a, 512)
                factor[2 * i + q] = scale[m] * scale[b]
                xa = spec[a].astype(jnp.float32)
                xb = spec[b].astype(jnp.float32)
                ra, ia, rb, ib = xa[:, :512], xa[:, 512:], xb[:, :512], xb[:, 512:]
                two.append(jnp.concatenate([ra * rb + ia * ib, ra * ib - ia * rb], axis=1))
            cross[i * 16 : i * 16 + 16, :] = jnp.concatenate(two, axis=0).astype(jnp.bfloat16)
        y = jnp.dot(cross[...], inverse[...], preferred_element_type=jnp.float32).reshape(CHUNK, 8, LAGS)
        f = factor[...]
        lo, hi = y[:, :, :LANES] * f, y[:, :, LANES:] * f
        span = pl.ds(t * CHUNK, CHUNK)
        tiles[span, :, :LANES] = lo.astype(jnp.bfloat16)
        tiles[span, :, LANES:] = hi.astype(jnp.bfloat16)
        top = jnp.max(jnp.maximum(lo, hi), axis=2, keepdims=True)
        g = t // (LANES // CHUNK)
        here = column == position + t % (LANES // CHUNK) * CHUNK
        peak_sum[0, g] += jnp.sum(jnp.where(here, top, 0.0), axis=0)
        peak_sum[1, g] += jnp.sum(jnp.where(here & (f > 0.0), 1.0, 0.0), axis=0)

        @pl.when(t % (LANES // CHUNK) == LANES // CHUNK - 1)
        def _():
            put(g).start()

    near, far = me % 8, me // 8

    def share(k, stage):
        to = far * 8 + (near + k) % 8 if stage == 0 else (far + k) % 8 * 8 + near
        return pltpu.make_async_remote_copy(
            src_ref=sums.at[stage],
            dst_ref=inbox.at[stage, k],
            send_sem=sum_send.at[stage, k],
            recv_sem=sum_recv.at[stage, k],
            device_id={"sta": to},
            device_id_type=MESH,
        )

    sums[0] = jnp.sum(peak_sum[...], axis=2)
    for stage in range(2):
        for k in range(1, 8):
            share(k, stage).start()
        total = sums[stage]
        for k in range(1, 8):
            share(k, stage).wait_recv()
            total = total + inbox[stage, k]
        if stage == 0:
            sums[1] = total
    mean_ref[...] = total[0] / jnp.maximum(total[1], 1.0)
    for stage in range(2):
        for k in range(1, 8):
            share(k, stage).wait_send()
    for g in range(8):
        put(g).wait()

    @pl.loop(1, 64)
    def _(k):
        send(k).wait_send()

    @pl.loop(0, 64)
    def _(k):
        forward(k).wait_send()


def body(waveforms, pair_events, pair_valid, presence):
    forward, inverse = spectral_tables(1024, LAGS)
    count = pair_events.shape[0]
    vmem = pl.BlockSpec(memory_space=pltpu.VMEM)
    smem = pl.BlockSpec(memory_space=pltpu.SMEM)
    hbm = pl.BlockSpec(memory_space=pl.ANY)
    correlation, mean = pl.pallas_call(
        kernel,
        out_shape=(
            jax.ShapeDtypeStruct((count, 8, LAGS), jnp.bfloat16),
            jax.ShapeDtypeStruct((8, LANES), jnp.float32),
        ),
        in_specs=[hbm, hbm, hbm, smem, smem, vmem],
        out_specs=(hbm, vmem),
        scratch_shapes=[
            pltpu.VMEM((128, 4, 8, 1024), jnp.bfloat16),
            pltpu.VMEM((1024, 1024), jnp.bfloat16),
            pltpu.VMEM((1024, LAGS), jnp.bfloat16),
            pltpu.VMEM((512, 8, 1024), jnp.bfloat16),
            pltpu.VMEM((520, 8, LANES), jnp.float32),
            pltpu.VMEM((CHUNK * 8, 1024), jnp.bfloat16),
            pltpu.VMEM((CHUNK, 8, LANES), jnp.float32),
            pltpu.VMEM((count, 8, LAGS), jnp.bfloat16),
            pltpu.VMEM((2, 8, 8, LANES), jnp.float32),
            pltpu.VMEM((2, 2, 8, LANES), jnp.float32),
            pltpu.VMEM((2, 8, 2, 8, LANES), jnp.float32),
            pltpu.SemaphoreType.DMA((64,)),
            pltpu.SemaphoreType.DMA((64,)),
            pltpu.SemaphoreType.DMA((64,)),
            pltpu.SemaphoreType.DMA((64,)),
            pltpu.SemaphoreType.DMA((3,)),
            pltpu.SemaphoreType.DMA((8,)),
            pltpu.SemaphoreType.DMA((2, 8)),
            pltpu.SemaphoreType.DMA((2, 8)),
        ],
        compiler_params=pltpu.CompilerParams(
            collective_id=0, has_side_effects=True, vmem_limit_bytes=60 << 20
        ),
    )(waveforms, jnp.asarray(forward), jnp.asarray(inverse), pair_events.T, pair_valid, presence.T)
    return (correlation, mean.reshape(count))


def solution(mesh):
    return jax.shard_map(
        body,
        mesh=mesh,
        in_specs=(P(("evt", "sta"), None, None), P("evt", None), P("evt"), P(None, "sta")),
        out_specs=(P("evt", "sta", None), P("evt")),
        check_vma=False,
    )
```

```python
import functools
import math

import jax
import jax.numpy as jnp
import numpy as np
from jax import lax
from jax.experimental import pallas as pl
from jax.experimental.pallas import tpu as pltpu
from jax.sharding import PartitionSpec as P

LAGS = 256
MESH = pl.DeviceIdType.MESH
LANES = 128


def spectral_tables(window, lag_count):
    half_width = window // 2
    bins = np.arange(half_width)
    phase = (np.arange(window)[:, None] * bins[None, :] % window) * (2.0 * math.pi / window)
    forward = np.concatenate([np.cos(phase), -np.sin(phase)], axis=1) / math.sqrt(window)
    shifts = np.arange(lag_count) - lag_count // 2
    angle = (bins[:, None] * shifts[None, :] % window) * (2.0 * math.pi / window)
    factor = np.where(bins == 0, 1.0, 2.0)[:, None]
    inverse = np.concatenate([factor * np.cos(angle), -factor * np.sin(angle)], axis=0)
    return forward.astype(np.float32).astype(jnp.bfloat16), inverse.astype(np.float32).astype(jnp.bfloat16)


CHUNK = 32


def kernel(
    w_ref, table_hbm, inverse_hbm, event_ref, valid_ref, presence_ref, out_ref, mean_ref,
    raw, table, inverse, spec, scale, cross, factor, peak_sum, sums, inbox, slot_a, slot_b, slot_m,
    send_sem, recv_sem, up_send, up_recv, local_sem, sum_send, sum_recv,
):
    me = lax.axis_index("sta")
    row = lax.axis_index("evt")
    rows = lax.axis_size("evt")
    z, x, c = me // 8, (me // 2) % 4, me % 2

    def target(k):
        dz, dx, dc = (3 * k) % 8, k // 16, (k // 8) % 2
        return ((z + dz) % 8) * 8 + ((x + dx) % 4) * 2 + (c + dc) % 2

    def source(k):
        dz, dx, dc = (3 * k) % 8, k // 16, (k // 8) % 2
        return ((z + 8 - dz) % 8) * 8 + ((x + 4 - dx) % 4) * 2 + (c + dc) % 2

    def send(k):
        to = target(k)
        return pltpu.make_async_remote_copy(
            src_ref=w_ref.at[:, pl.ds(pl.multiple_of(to * 8, 8), 8), :],
            dst_ref=raw.at[me],
            send_sem=send_sem.at[0],
            recv_sem=recv_sem.at[k],
            device_id={"sta": to},
            device_id_type=MESH,
        )

    def forward(k):
        s = source(k)
        side = jnp.where(s < 32, rows - 1, 1)
        return pltpu.make_async_remote_copy(
            src_ref=raw.at[s],
            dst_ref=raw.at[64 + s],
            send_sem=up_send.at[0],
            recv_sem=up_recv.at[k // 8],
            device_id={"evt": (row + side) % rows},
            device_id_type=MESH,
        )

    fetch = pltpu.make_async_copy(table_hbm, table, local_sem.at[0])
    fetch.start()
    own = pltpu.make_async_copy(
        w_ref.at[:, pl.ds(pl.multiple_of(me * 8, 8), 8), :], raw.at[me], local_sem.at[1]
    )
    own.start()
    fetch_inverse = pltpu.make_async_copy(inverse_hbm, inverse, local_sem.at[2])
    fetch_inverse.start()
    barrier = pltpu.get_barrier_semaphore()

    @pl.loop(1, 64)
    def _(k):
        pl.semaphore_signal(barrier, inc=1, device_id={"sta": target(k)}, device_id_type=MESH)

    for side in (1, rows - 1):
        pl.semaphore_signal(
            barrier, inc=1, device_id={"evt": (row + side) % rows}, device_id_type=MESH
        )
    pl.semaphore_wait(barrier, 65)

    @pl.loop(1, 64)
    def _(k):
        send(k).start()

    first_event = row * 256
    events = rows * 256
    lane_one = lax.broadcasted_iota(jnp.int32, (8, LANES), 1)

    @pl.loop(0, 128)
    def _(s):
        shift = jnp.where(s < 64, 0, jnp.where(s < 96, 0, -512))
        event = (first_event + events + shift + 4 * s) % events
        tile = presence_ref[:, pl.ds(pl.multiple_of(event // LANES * LANES, LANES), LANES)].astype(jnp.float32)
        for e in range(4):
            here = jnp.where(lane_one == event % LANES + e, tile, 0.0)
            scale[s * 4 + e] = jnp.broadcast_to(jnp.sum(here, axis=1, keepdims=True), (8, LANES))

    scale[pl.ds(512, 8)] = jnp.zeros((8, 8, LANES), jnp.float32)

    def slots_of(p):
        a = (event_ref[0, p] - first_event) & 511
        b = (event_ref[1, p] - first_event) & 511
        return a, b, jnp.where(valid_ref[p] == 1, a, 512)

    @pl.loop(0, 8)
    def _(g):
        def some(i, total):
            for q in range(8):
                p = g * LANES + i * 8 + q
                a, b, m = slots_of(p)
                slot_a[p] = a
                slot_b[p] = b
                slot_m[p] = m
                total = total + jnp.where(lane_one == i * 8 + q, scale[m] * scale[b], 0.0)
            return total

        total = lax.fori_loop(0, LANES // 8, some, jnp.zeros((8, LANES), jnp.float32))
        sums[0, 1, pl.ds(g, 1), :] = jnp.sum(total, axis=0, keepdims=True)

    lane = lax.broadcasted_iota(jnp.int32, (1, 256), 1)

    def transform(slots):
        block = jnp.concatenate([raw[s].reshape(32, 1024) for s in slots], axis=0)
        power = jnp.zeros((256, LANES), jnp.float32)
        for n in range(4):
            y = jnp.dot(block, table[:, n * 256 : (n + 1) * 256], preferred_element_type=jnp.float32)
            y = y.astype(jnp.bfloat16)
            for i, s in enumerate(slots):
                spec[pl.ds(s * 4, 4), :, n * 256 : (n + 1) * 256] = y[i * 32 : i * 32 + 32].reshape(4, 8, 256)
            y = y.astype(jnp.float32)
            weight = 2.0 if n % 2 else jnp.where(lane == 0, 1.0, 2.0)
            y = y * y * weight
            power = power + y[:, :LANES] + y[:, LANES:]
        energy = jnp.sum(power, axis=1, keepdims=True) + 1e-06
        strength = jnp.broadcast_to(lax.rsqrt(energy), (256, LANES)).reshape(8, 4, 8, LANES)
        for i, s in enumerate(slots):
            scale[pl.ds(s * 4, 4)] = scale[pl.ds(s * 4, 4)] * strength[i]

    def own_batch(j):
        transform([source(8 * j + i) for i in range(8)])

    def halo_batch(j):
        pltpu.make_async_copy(raw.at[pl.ds(0, 8)], raw.at[pl.ds(64, 8)], up_recv.at[j]).wait()
        transform([64 + source(8 * j + i) for i in range(8)])

    fetch.wait()
    fetch_inverse.wait()

    @pl.loop(0, 8)
    def _(j):
        @pl.loop(0, 8)
        def _(i):
            k = 8 * j + i

            @pl.when(k == 0)
            def _():
                own.wait()

            @pl.when(k > 0)
            def _():
                send(k).wait_recv()

            forward(k).start()

        own_batch(j)

        @pl.when(j > 0)
        def _():
            halo_batch(j - 1)

    halo_batch(7)

    column = lax.broadcasted_iota(jnp.int32, (1, 1, LANES), 2)
    position = lax.broadcasted_iota(jnp.int32, (CHUNK, 1, 1), 0)
    chunks = 1024 // CHUNK
    in_row = LANES // CHUNK
    peak_sum[...] = jnp.zeros_like(peak_sum)

    def multiply(t, cross, factor):
        for i in range(CHUNK // 2):
            two = []
            for q in range(2):
                p = t * CHUNK + 2 * i + q
                b = slot_b[p]
                factor[2 * i + q] = scale[slot_m[p]] * scale[b]
                xa, xb = spec[slot_a[p]], spec[b]
                ra, ia, rb, ib = xa[:, :512], xa[:, 512:], xb[:, :512], xb[:, 512:]
                two.append(jnp.concatenate([ra * rb + ia * ib, ra * ib - ia * rb], axis=1))
            cross[i * 16 : i * 16 + 16, :] = jnp.concatenate(two, axis=0)

    def correlate(t, cross, factor):
        y = jnp.dot(cross[...], inverse[...], preferred_element_type=jnp.float32).reshape(CHUNK, 8, LAGS)
        f = factor[...]
        lo, hi = y[:, :, :LANES] * f, y[:, :, LANES:] * f
        span = pl.ds(t * CHUNK, CHUNK)
        out_ref[span] = jnp.concatenate([lo, hi], axis=2).astype(jnp.bfloat16)
        top = jnp.max(jnp.maximum(lo, hi), axis=2, keepdims=True)
        here = column == position + t % in_row * CHUNK
        peak_sum[t // in_row] += jnp.sum(jnp.where(here, top, 0.0), axis=0)

    @pl.loop(0, chunks // 4)
    def _(u):
        for v in range(4):
            multiply(4 * u + v, cross.at[v], factor.at[v])
        for v in range(4):
            correlate(4 * u + v, cross.at[v], factor.at[v])

    near, far = me % 8, me // 8

    def share(k, stage):
        to = far * 8 + (near + k) % 8 if stage == 0 else (far + k) % 8 * 8 + near
        return pltpu.make_async_remote_copy(
            src_ref=sums.at[stage],
            dst_ref=inbox.at[stage, k],
            send_sem=sum_send.at[stage, k],
            recv_sem=sum_recv.at[stage, k],
            device_id={"sta": to},
            device_id_type=MESH,
        )

    sums[0, 0] = jnp.sum(peak_sum[...], axis=1)
    for stage in range(2):
        for k in range(1, 8):
            share(k, stage).start()
        total = sums[stage]
        for k in range(1, 8):
            share(k, stage).wait_recv()
            total = total + inbox[stage, k]
        if stage == 0:
            sums[1] = total
    mean_ref[...] = total[0] / jnp.maximum(total[1], 1.0)
    for stage in range(2):
        for k in range(1, 8):
            share(k, stage).wait_send()
    pltpu.make_async_copy(raw.at[pl.ds(0, 63)], raw.at[pl.ds(64, 63)], send_sem.at[0]).wait()
    pltpu.make_async_copy(raw.at[pl.ds(0, 64)], raw.at[pl.ds(64, 64)], up_send.at[0]).wait()


def body(waveforms, pair_events, pair_valid, presence):
    forward, inverse = spectral_tables(1024, LAGS)
    count = pair_events.shape[0]
    vmem = pl.BlockSpec(memory_space=pltpu.VMEM)
    smem = pl.BlockSpec(memory_space=pltpu.SMEM)
    hbm = pl.BlockSpec(memory_space=pltpu.HBM)
    correlation, mean = pl.pallas_call(
        kernel,
        out_shape=(
            jax.ShapeDtypeStruct((count, 8, LAGS), jnp.bfloat16),
            jax.ShapeDtypeStruct((8, LANES), jnp.float32),
        ),
        in_specs=[hbm, hbm, hbm, smem, smem, vmem],
        out_specs=(vmem, vmem),
        scratch_shapes=[
            pltpu.VMEM((128, 4, 8, 1024), jnp.bfloat16),
            pltpu.VMEM((1024, 1024), jnp.bfloat16),
            pltpu.VMEM((1024, LAGS), jnp.bfloat16),
            pltpu.VMEM((512, 8, 1024), jnp.bfloat16),
            pltpu.VMEM((520, 8, LANES), jnp.float32),
            pltpu.VMEM((4, CHUNK * 8, 1024), jnp.bfloat16),
            pltpu.VMEM((4, CHUNK, 8, LANES), jnp.float32),
            pltpu.VMEM((8, 8, LANES), jnp.float32),
            pltpu.VMEM((2, 2, 8, LANES), jnp.float32),
            pltpu.VMEM((2, 8, 2, 8, LANES), jnp.float32),
            pltpu.SMEM((count,), jnp.int32),
            pltpu.SMEM((count,), jnp.int32),
            pltpu.SMEM((count,), jnp.int32),
            pltpu.SemaphoreType.DMA((1,)),
            pltpu.SemaphoreType.DMA((64,)),
            pltpu.SemaphoreType.DMA((1,)),
            pltpu.SemaphoreType.DMA((8,)),
            pltpu.SemaphoreType.DMA((3,)),
            pltpu.SemaphoreType.DMA((2, 8)),
            pltpu.SemaphoreType.DMA((2, 8)),
        ],
        compiler_params=pltpu.CompilerParams(
            collective_id=0, has_side_effects=True, vmem_limit_bytes=44 << 20
        ),
    )(*(pltpu.with_memory_space_constraint(v, pltpu.HBM) for v in (waveforms, jnp.asarray(forward), jnp.asarray(inverse))), pair_events.T, pair_valid, presence.T)
    return (correlation, mean.reshape(count))


def solution(mesh):
    return jax.shard_map(
        body,
        mesh=mesh,
        in_specs=(P(("evt", "sta"), None, None), P("evt", None), P("evt"), P(None, "sta")),
        out_specs=(P("evt", "sta", None), P("evt")),
        check_vma=False,
    )
```

```python
import functools
import math

import jax
import jax.numpy as jnp
import numpy as np
from jax import lax
from jax.experimental import pallas as pl
from jax.experimental.pallas import tpu as pltpu
from jax.sharding import PartitionSpec as P

LAGS = 256
MESH = pl.DeviceIdType.MESH
LANES = 128


def spectral_tables(window, lag_count):
    half_width = window // 2
    bins = np.arange(half_width)
    phase = (np.arange(window)[:, None] * bins[None, :] % window) * (2.0 * math.pi / window)
    forward = np.concatenate([np.cos(phase), -np.sin(phase)], axis=1) / math.sqrt(window)
    shifts = np.arange(lag_count) - lag_count // 2
    angle = (bins[:, None] * shifts[None, :] % window) * (2.0 * math.pi / window)
    factor = np.where(bins == 0, 1.0, 2.0)[:, None]
    inverse = np.concatenate([factor * np.cos(angle), -factor * np.sin(angle)], axis=0)
    return forward.astype(np.float32).astype(jnp.bfloat16), inverse.astype(np.float32).astype(jnp.bfloat16)


CHUNK = 32


def kernel(
    w_ref, table_hbm, inverse_hbm, event_ref, valid_ref, presence_ref, out_ref, mean_ref,
    raw, table, inverse, spec, scale, cross, factor, peak_sum, sums, inbox, slot_a, slot_b, slot_m,
    send_sem, recv_sem, up_send, up_recv, local_sem, sum_send, sum_recv,
):
    me = lax.axis_index("sta")
    row = lax.axis_index("evt")
    rows = lax.axis_size("evt")
    z, x, c = me // 8, (me // 2) % 4, me % 2

    def target(k):
        dz, dx, dc = (5 * k) % 8, (k // 16 + k) % 4, (k // 8 + k // 2) % 2
        return ((z + dz) % 8) * 8 + ((x + dx) % 4) * 2 + (c + dc) % 2

    def source(k):
        dz, dx, dc = (5 * k) % 8, (k // 16 + k) % 4, (k // 8 + k // 2) % 2
        return ((z + 8 - dz) % 8) * 8 + ((x + 4 - dx) % 4) * 2 + (c + dc) % 2

    def send(k):
        to = target(k)
        return pltpu.make_async_remote_copy(
            src_ref=w_ref.at[:, pl.ds(pl.multiple_of(to * 8, 8), 8), :],
            dst_ref=raw.at[me],
            send_sem=send_sem.at[0],
            recv_sem=recv_sem.at[k],
            device_id={"sta": to},
            device_id_type=MESH,
        )

    def forward(k):
        s = source(k)
        side = jnp.where(s < 32, rows - 1, 1)
        return pltpu.make_async_remote_copy(
            src_ref=raw.at[s],
            dst_ref=raw.at[64 + s],
            send_sem=up_send.at[0],
            recv_sem=up_recv.at[k // 8],
            device_id={"evt": (row + side) % rows},
            device_id_type=MESH,
        )

    fetch = pltpu.make_async_copy(table_hbm, table, local_sem.at[0])
    fetch.start()
    own = pltpu.make_async_copy(
        w_ref.at[:, pl.ds(pl.multiple_of(me * 8, 8), 8), :], raw.at[me], local_sem.at[1]
    )
    own.start()
    fetch_inverse = pltpu.make_async_copy(inverse_hbm, inverse, local_sem.at[2])
    fetch_inverse.start()
    barrier = pltpu.get_barrier_semaphore()

    @pl.loop(1, 64)
    def _(k):
        pl.semaphore_signal(barrier, inc=1, device_id={"sta": target(k)}, device_id_type=MESH)

    for side in (1, rows - 1):
        pl.semaphore_signal(
            barrier, inc=1, device_id={"evt": (row + side) % rows}, device_id_type=MESH
        )
    pl.semaphore_wait(barrier, 65)

    @pl.loop(1, 64)
    def _(k):
        send(k).start()

    first_event = row * 256
    events = rows * 256
    lane_one = lax.broadcasted_iota(jnp.int32, (8, LANES), 1)

    @pl.loop(0, 128)
    def _(s):
        shift = jnp.where(s < 64, 0, jnp.where(s < 96, 0, -512))
        event = (first_event + events + shift + 4 * s) % events
        tile = presence_ref[:, pl.ds(pl.multiple_of(event // LANES * LANES, LANES), LANES)].astype(jnp.float32)
        for e in range(4):
            here = jnp.where(lane_one == event % LANES + e, tile, 0.0)
            scale[s * 4 + e] = jnp.broadcast_to(jnp.sum(here, axis=1, keepdims=True), (8, LANES))

    scale[pl.ds(512, 8)] = jnp.zeros((8, 8, LANES), jnp.float32)

    def slots_of(p):
        a = (event_ref[0, p] - first_event) & 511
        b = (event_ref[1, p] - first_event) & 511
        return a, b, jnp.where(valid_ref[p] == 1, a, 512)

    @pl.loop(0, 8)
    def _(g):
        def some(i, total):
            for q in range(8):
                p = g * LANES + i * 8 + q
                a, b, m = slots_of(p)
                slot_a[p] = a
                slot_b[p] = b
                slot_m[p] = m
                total = total + jnp.where(lane_one == i * 8 + q, scale[m] * scale[b], 0.0)
            return total

        total = lax.fori_loop(0, LANES // 8, some, jnp.zeros((8, LANES), jnp.float32))
        sums[0, 1, pl.ds(g, 1), :] = jnp.sum(total, axis=0, keepdims=True)

    lane = lax.broadcasted_iota(jnp.int32, (1, 256), 1)

    def transform(slots):
        block = jnp.concatenate([raw[s].reshape(32, 1024) for s in slots], axis=0)
        power = jnp.zeros((256, LANES), jnp.float32)
        for n in range(4):
            y = jnp.dot(block, table[:, n * 256 : (n + 1) * 256], preferred_element_type=jnp.float32)
            y = y.astype(jnp.bfloat16)
            for i, s in enumerate(slots):
                spec[pl.ds(s * 4, 4), :, n * 256 : (n + 1) * 256] = y[i * 32 : i * 32 + 32].reshape(4, 8, 256)
            y = y.astype(jnp.float32)
            weight = 2.0 if n % 2 else jnp.where(lane == 0, 1.0, 2.0)
            y = y * y * weight
            power = power + y[:, :LANES] + y[:, LANES:]
        energy = jnp.sum(power, axis=1, keepdims=True) + 1e-06
        strength = jnp.broadcast_to(lax.rsqrt(energy), (256, LANES)).reshape(8, 4, 8, LANES)
        for i, s in enumerate(slots):
            scale[pl.ds(s * 4, 4)] = scale[pl.ds(s * 4, 4)] * strength[i]

    def own_batch(j):
        transform([source(8 * j + i) for i in range(8)])

    def halo_batch(j):
        pltpu.make_async_copy(raw.at[pl.ds(0, 8)], raw.at[pl.ds(64, 8)], up_recv.at[j]).wait()
        transform([64 + source(8 * j + i) for i in range(8)])

    fetch.wait()
    fetch_inverse.wait()

    @pl.loop(0, 8)
    def _(j):
        @pl.loop(0, 8)
        def _(i):
            k = 8 * j + i

            @pl.when(k == 0)
            def _():
                own.wait()

            @pl.when(k > 0)
            def _():
                send(k).wait_recv()

            forward(k).start()

        own_batch(j)

        @pl.when(j > 0)
        def _():
            halo_batch(j - 1)

    halo_batch(7)

    column = lax.broadcasted_iota(jnp.int32, (1, 1, LANES), 2)
    position = lax.broadcasted_iota(jnp.int32, (CHUNK, 1, 1), 0)
    chunks = 1024 // CHUNK
    in_row = LANES // CHUNK
    peak_sum[...] = jnp.zeros_like(peak_sum)

    def multiply(t, cross, factor):
        for i in range(CHUNK // 2):
            two = []
            for q in range(2):
                p = t * CHUNK + 2 * i + q
                b = slot_b[p]
                factor[2 * i + q] = scale[slot_m[p]] * scale[b]
                xa, xb = spec[slot_a[p]], spec[b]
                ra, ia, rb, ib = xa[:, :512], xa[:, 512:], xb[:, :512], xb[:, 512:]
                two.append(jnp.concatenate([ra * rb + ia * ib, ra * ib - ia * rb], axis=1))
            cross[i * 16 : i * 16 + 16, :] = jnp.concatenate(two, axis=0)

    def correlate(t, cross, factor):
        y = jnp.dot(cross[...], inverse[...], preferred_element_type=jnp.float32).reshape(CHUNK, 8, LAGS)
        f = factor[...]
        lo, hi = y[:, :, :LANES] * f, y[:, :, LANES:] * f
        span = pl.ds(t * CHUNK, CHUNK)
        out_ref[span] = jnp.concatenate([lo, hi], axis=2).astype(jnp.bfloat16)
        top = jnp.max(jnp.maximum(lo, hi), axis=2, keepdims=True)
        here = column == position + t % in_row * CHUNK
        peak_sum[t // in_row] += jnp.sum(jnp.where(here, top, 0.0), axis=0)

    @pl.loop(0, chunks // 4)
    def _(u):
        for v in range(4):
            multiply(4 * u + v, cross.at[v], factor.at[v])
        for v in range(4):
            correlate(4 * u + v, cross.at[v], factor.at[v])

    near, far = me % 8, me // 8

    def share(k, stage):
        to = far * 8 + (near + k) % 8 if stage == 0 else (far + k) % 8 * 8 + near
        return pltpu.make_async_remote_copy(
            src_ref=sums.at[stage],
            dst_ref=inbox.at[stage, k],
            send_sem=sum_send.at[stage, k],
            recv_sem=sum_recv.at[stage, k],
            device_id={"sta": to},
            device_id_type=MESH,
        )

    sums[0, 0] = jnp.sum(peak_sum[...], axis=1)
    for stage in range(2):
        for k in range(1, 8):
            share(k, stage).start()
        total = sums[stage]
        for k in range(1, 8):
            share(k, stage).wait_recv()
            total = total + inbox[stage, k]
        if stage == 0:
            sums[1] = total
    mean_ref[...] = total[0] / jnp.maximum(total[1], 1.0)
    for stage in range(2):
        for k in range(1, 8):
            share(k, stage).wait_send()
    pltpu.make_async_copy(raw.at[pl.ds(0, 63)], raw.at[pl.ds(64, 63)], send_sem.at[0]).wait()
    pltpu.make_async_copy(raw.at[pl.ds(0, 64)], raw.at[pl.ds(64, 64)], up_send.at[0]).wait()


def body(waveforms, pair_events, pair_valid, presence):
    forward, inverse = spectral_tables(1024, LAGS)
    count = pair_events.shape[0]
    vmem = pl.BlockSpec(memory_space=pltpu.VMEM)
    smem = pl.BlockSpec(memory_space=pltpu.SMEM)
    hbm = pl.BlockSpec(memory_space=pltpu.HBM)
    correlation, mean = pl.pallas_call(
        kernel,
        out_shape=(
            jax.ShapeDtypeStruct((count, 8, LAGS), jnp.bfloat16),
            jax.ShapeDtypeStruct((8, LANES), jnp.float32),
        ),
        in_specs=[hbm, hbm, hbm, smem, smem, vmem],
        out_specs=(vmem, vmem),
        scratch_shapes=[
            pltpu.VMEM((128, 4, 8, 1024), jnp.bfloat16),
            pltpu.VMEM((1024, 1024), jnp.bfloat16),
            pltpu.VMEM((1024, LAGS), jnp.bfloat16),
            pltpu.VMEM((512, 8, 1024), jnp.bfloat16),
            pltpu.VMEM((520, 8, LANES), jnp.float32),
            pltpu.VMEM((4, CHUNK * 8, 1024), jnp.bfloat16),
            pltpu.VMEM((4, CHUNK, 8, LANES), jnp.float32),
            pltpu.VMEM((8, 8, LANES), jnp.float32),
            pltpu.VMEM((2, 2, 8, LANES), jnp.float32),
            pltpu.VMEM((2, 8, 2, 8, LANES), jnp.float32),
            pltpu.SMEM((count,), jnp.int32),
            pltpu.SMEM((count,), jnp.int32),
            pltpu.SMEM((count,), jnp.int32),
            pltpu.SemaphoreType.DMA((1,)),
            pltpu.SemaphoreType.DMA((64,)),
            pltpu.SemaphoreType.DMA((1,)),
            pltpu.SemaphoreType.DMA((8,)),
            pltpu.SemaphoreType.DMA((3,)),
            pltpu.SemaphoreType.DMA((2, 8)),
            pltpu.SemaphoreType.DMA((2, 8)),
        ],
        compiler_params=pltpu.CompilerParams(
            collective_id=0, has_side_effects=True, vmem_limit_bytes=44 << 20
        ),
    )(*(pltpu.with_memory_space_constraint(v, pltpu.HBM) for v in (waveforms, jnp.asarray(forward), jnp.asarray(inverse))), pair_events.T, pair_valid, presence.T)
    return (correlation, mean.reshape(count))


def solution(mesh):
    return jax.shard_map(
        body,
        mesh=mesh,
        in_specs=(P(("evt", "sta"), None, None), P("evt", None), P("evt"), P(None, "sta")),
        out_specs=(P("evt", "sta", None), P("evt")),
        check_vma=False,
    )
```

```python
import functools
import math

import jax
import jax.numpy as jnp
import numpy as np
from jax import lax
from jax.experimental import pallas as pl
from jax.experimental.pallas import tpu as pltpu
from jax.sharding import PartitionSpec as P

LAGS = 256
MESH = pl.DeviceIdType.MESH
LANES = 128


def spectral_tables(window, lag_count):
    half_width = window // 2
    bins = np.arange(half_width)
    phase = (np.arange(window)[:, None] * bins[None, :] % window) * (2.0 * math.pi / window)
    forward = np.concatenate([np.cos(phase), -np.sin(phase)], axis=1) / math.sqrt(window)
    shifts = np.arange(lag_count) - lag_count // 2
    angle = (bins[:, None] * shifts[None, :] % window) * (2.0 * math.pi / window)
    factor = np.where(bins == 0, 1.0, 2.0)[:, None]
    inverse = np.concatenate([factor * np.cos(angle), -factor * np.sin(angle)], axis=0)
    return forward.astype(np.float32).astype(jnp.bfloat16), inverse.astype(np.float32).astype(jnp.bfloat16)


CHUNK = 32


def kernel(
    w_ref, table_hbm, inverse_hbm, event_ref, valid_ref, presence_ref, out_ref, mean_ref,
    raw, table, inverse, spec, scale, cross, factor, peak_sum, sums, inbox, slot_a, slot_b, slot_m,
    send_sem, recv_sem, up_send, up_recv, local_sem, sum_send, sum_recv,
):
    me = lax.axis_index("sta")
    row = lax.axis_index("evt")
    rows = lax.axis_size("evt")
    z, x, c = me // 8, (me // 2) % 4, me % 2

    def target(k):
        dz, dx, dc = lax.shift_right_logical(jnp.int32(13287008), 3 * (k % 8)) % 8, (k // 16 + k) % 4, (k // 8 + k // 2) % 2
        return ((z + dz) % 8) * 8 + ((x + dx) % 4) * 2 + (c + dc) % 2

    def source(k):
        dz, dx, dc = lax.shift_right_logical(jnp.int32(13287008), 3 * (k % 8)) % 8, (k // 16 + k) % 4, (k // 8 + k // 2) % 2
        return ((z + 8 - dz) % 8) * 8 + ((x + 4 - dx) % 4) * 2 + (c + dc) % 2

    def send(k):
        to = target(k)
        return pltpu.make_async_remote_copy(
            src_ref=w_ref.at[:, pl.ds(pl.multiple_of(to * 8, 8), 8), :],
            dst_ref=raw.at[me],
            send_sem=send_sem.at[0],
            recv_sem=recv_sem.at[k],
            device_id={"sta": to},
            device_id_type=MESH,
        )

    def forward(k):
        s = source(k)
        side = jnp.where(s < 32, rows - 1, 1)
        return pltpu.make_async_remote_copy(
            src_ref=raw.at[s],
            dst_ref=raw.at[64 + s],
            send_sem=up_send.at[0],
            recv_sem=up_recv.at[k // 8],
            device_id={"evt": (row + side) % rows},
            device_id_type=MESH,
        )

    fetch = pltpu.make_async_copy(table_hbm, table, local_sem.at[0])
    fetch.start()
    own = pltpu.make_async_copy(
        w_ref.at[:, pl.ds(pl.multiple_of(me * 8, 8), 8), :], raw.at[me], local_sem.at[1]
    )
    own.start()
    fetch_inverse = pltpu.make_async_copy(inverse_hbm, inverse, local_sem.at[2])
    fetch_inverse.start()
    barrier = pltpu.get_barrier_semaphore()

    @pl.loop(1, 64)
    def _(k):
        pl.semaphore_signal(barrier, inc=1, device_id={"sta": target(k)}, device_id_type=MESH)

    for side in (1, rows - 1):
        pl.semaphore_signal(
            barrier, inc=1, device_id={"evt": (row + side) % rows}, device_id_type=MESH
        )
    pl.semaphore_wait(barrier, 65)

    @pl.loop(1, 64)
    def _(k):
        send(k).start()

    first_event = row * 256
    events = rows * 256
    lane_one = lax.broadcasted_iota(jnp.int32, (8, LANES), 1)

    @pl.loop(0, 128)
    def _(s):
        shift = jnp.where(s < 64, 0, jnp.where(s < 96, 0, -512))
        event = (first_event + events + shift + 4 * s) % events
        tile = presence_ref[:, pl.ds(pl.multiple_of(event // LANES * LANES, LANES), LANES)].astype(jnp.float32)
        for e in range(4):
            here = jnp.where(lane_one == event % LANES + e, tile, 0.0)
            scale[s * 4 + e] = jnp.broadcast_to(jnp.sum(here, axis=1, keepdims=True), (8, LANES))

    scale[pl.ds(512, 8)] = jnp.zeros((8, 8, LANES), jnp.float32)

    def slots_of(p):
        a = (event_ref[0, p] - first_event) & 511
        b = (event_ref[1, p] - first_event) & 511
        return a, b, jnp.where(valid_ref[p] == 1, a, 512)

    @pl.loop(0, 8)
    def _(g):
        def some(i, total):
            for q in range(8):
                p = g * LANES + i * 8 + q
                a, b, m = slots_of(p)
                slot_a[p] = a
                slot_b[p] = b
                slot_m[p] = m
                total = total + jnp.where(lane_one == i * 8 + q, scale[m] * scale[b], 0.0)
            return total

        total = lax.fori_loop(0, LANES // 8, some, jnp.zeros((8, LANES), jnp.float32))
        sums[0, 1, pl.ds(g, 1), :] = jnp.sum(total, axis=0, keepdims=True)

    lane = lax.broadcasted_iota(jnp.int32, (1, 256), 1)

    def transform(slots):
        block = jnp.concatenate([raw[s].reshape(32, 1024) for s in slots], axis=0)
        power = jnp.zeros((256, LANES), jnp.float32)
        for n in range(4):
            y = jnp.dot(block, table[:, n * 256 : (n + 1) * 256], preferred_element_type=jnp.float32)
            y = y.astype(jnp.bfloat16)
            for i, s in enumerate(slots):
                spec[pl.ds(s * 4, 4), :, n * 256 : (n + 1) * 256] = y[i * 32 : i * 32 + 32].reshape(4, 8, 256)
            y = y.astype(jnp.float32)
            weight = 2.0 if n % 2 else jnp.where(lane == 0, 1.0, 2.0)
            y = y * y * weight
            power = power + y[:, :LANES] + y[:, LANES:]
        energy = jnp.sum(power, axis=1, keepdims=True) + 1e-06
        strength = jnp.broadcast_to(lax.rsqrt(energy), (256, LANES)).reshape(8, 4, 8, LANES)
        for i, s in enumerate(slots):
            scale[pl.ds(s * 4, 4)] = scale[pl.ds(s * 4, 4)] * strength[i]

    def own_batch(j):
        transform([source(8 * j + i) for i in range(8)])

    def halo_batch(j):
        pltpu.make_async_copy(raw.at[pl.ds(0, 8)], raw.at[pl.ds(64, 8)], up_recv.at[j]).wait()
        transform([64 + source(8 * j + i) for i in range(8)])

    fetch.wait()
    fetch_inverse.wait()

    @pl.loop(0, 8)
    def _(j):
        @pl.loop(0, 8)
        def _(i):
            k = 8 * j + i

            @pl.when(k == 0)
            def _():
                own.wait()

            @pl.when(k > 0)
            def _():
                send(k).wait_recv()

            forward(k).start()

        own_batch(j)

        @pl.when(j > 0)
        def _():
            halo_batch(j - 1)

    halo_batch(7)

    column = lax.broadcasted_iota(jnp.int32, (1, 1, LANES), 2)
    position = lax.broadcasted_iota(jnp.int32, (CHUNK, 1, 1), 0)
    chunks = 1024 // CHUNK
    in_row = LANES // CHUNK
    peak_sum[...] = jnp.zeros_like(peak_sum)

    def multiply(t, cross, factor):
        for i in range(CHUNK // 2):
            two = []
            for q in range(2):
                p = t * CHUNK + 2 * i + q
                b = slot_b[p]
                factor[2 * i + q] = scale[slot_m[p]] * scale[b]
                xa, xb = spec[slot_a[p]], spec[b]
                ra, ia, rb, ib = xa[:, :512], xa[:, 512:], xb[:, :512], xb[:, 512:]
                two.append(jnp.concatenate([ra * rb + ia * ib, ra * ib - ia * rb], axis=1))
            cross[i * 16 : i * 16 + 16, :] = jnp.concatenate(two, axis=0)

    def correlate(t, cross, factor):
        y = jnp.dot(cross[...], inverse[...], preferred_element_type=jnp.float32).reshape(CHUNK, 8, LAGS)
        f = factor[...]
        lo, hi = y[:, :, :LANES] * f, y[:, :, LANES:] * f
        span = pl.ds(t * CHUNK, CHUNK)
        out_ref[span] = jnp.concatenate([lo, hi], axis=2).astype(jnp.bfloat16)
        top = jnp.max(jnp.maximum(lo, hi), axis=2, keepdims=True)
        here = column == position + t % in_row * CHUNK
        peak_sum[t // in_row] += jnp.sum(jnp.where(here, top, 0.0), axis=0)

    @pl.loop(0, chunks // 8)
    def _(u):
        for v in range(8):
            multiply(8 * u + v, cross.at[v], factor.at[v])
        for v in range(8):
            correlate(8 * u + v, cross.at[v], factor.at[v])

    near, far = me % 8, me // 8

    def share(k, stage):
        to = far * 8 + (near + k) % 8 if stage == 0 else (far + k) % 8 * 8 + near
        return pltpu.make_async_remote_copy(
            src_ref=sums.at[stage],
            dst_ref=inbox.at[stage, k],
            send_sem=sum_send.at[stage, k],
            recv_sem=sum_recv.at[stage, k],
            device_id={"sta": to},
            device_id_type=MESH,
        )

    sums[0, 0] = jnp.sum(peak_sum[...], axis=1)
    for stage in range(2):
        for k in range(1, 8):
            share(k, stage).start()
        total = sums[stage]
        for k in range(1, 8):
            share(k, stage).wait_recv()
            total = total + inbox[stage, k]
        if stage == 0:
            sums[1] = total
    mean_ref[...] = total[0] / jnp.maximum(total[1], 1.0)
    for stage in range(2):
        for k in range(1, 8):
            share(k, stage).wait_send()
    pltpu.make_async_copy(raw.at[pl.ds(0, 63)], raw.at[pl.ds(64, 63)], send_sem.at[0]).wait()
    pltpu.make_async_copy(raw.at[pl.ds(0, 64)], raw.at[pl.ds(64, 64)], up_send.at[0]).wait()


def body(waveforms, pair_events, pair_valid, presence):
    forward, inverse = spectral_tables(1024, LAGS)
    count = pair_events.shape[0]
    vmem = pl.BlockSpec(memory_space=pltpu.VMEM)
    smem = pl.BlockSpec(memory_space=pltpu.SMEM)
    hbm = pl.BlockSpec(memory_space=pltpu.HBM)
    correlation, mean = pl.pallas_call(
        kernel,
        out_shape=(
            jax.ShapeDtypeStruct((count, 8, LAGS), jnp.bfloat16),
            jax.ShapeDtypeStruct((8, LANES), jnp.float32),
        ),
        in_specs=[hbm, hbm, hbm, smem, smem, vmem],
        out_specs=(vmem, vmem),
        scratch_shapes=[
            pltpu.VMEM((128, 4, 8, 1024), jnp.bfloat16),
            pltpu.VMEM((1024, 1024), jnp.bfloat16),
            pltpu.VMEM((1024, LAGS), jnp.bfloat16),
            pltpu.VMEM((512, 8, 1024), jnp.bfloat16),
            pltpu.VMEM((520, 8, LANES), jnp.float32),
            pltpu.VMEM((8, CHUNK * 8, 1024), jnp.bfloat16),
            pltpu.VMEM((8, CHUNK, 8, LANES), jnp.float32),
            pltpu.VMEM((8, 8, LANES), jnp.float32),
            pltpu.VMEM((2, 2, 8, LANES), jnp.float32),
            pltpu.VMEM((2, 8, 2, 8, LANES), jnp.float32),
            pltpu.SMEM((count,), jnp.int32),
            pltpu.SMEM((count,), jnp.int32),
            pltpu.SMEM((count,), jnp.int32),
            pltpu.SemaphoreType.DMA((1,)),
            pltpu.SemaphoreType.DMA((64,)),
            pltpu.SemaphoreType.DMA((1,)),
            pltpu.SemaphoreType.DMA((8,)),
            pltpu.SemaphoreType.DMA((3,)),
            pltpu.SemaphoreType.DMA((2, 8)),
            pltpu.SemaphoreType.DMA((2, 8)),
        ],
        compiler_params=pltpu.CompilerParams(
            collective_id=0, has_side_effects=True, vmem_limit_bytes=44 << 20
        ),
    )(*(pltpu.with_memory_space_constraint(v, pltpu.HBM) for v in (waveforms, jnp.asarray(forward), jnp.asarray(inverse))), pair_events.T, pair_valid, presence.T)
    return (correlation, mean.reshape(count))


def solution(mesh):
    return jax.shard_map(
        body,
        mesh=mesh,
        in_specs=(P(("evt", "sta"), None, None), P("evt", None), P("evt"), P(None, "sta")),
        out_specs=(P("evt", "sta", None), P("evt")),
        check_vma=False,
    )
```
